32 devices in a mesh: win: 2 (over x), row: 16 (over z, y, core).
Axes of the slice: x: 2, y: 2, z: 4, core: 2. Of those that a mesh axis runs over, the one named last changes fastest.
Arguments:
- mask_field: float32 [2, 4096, 128], P(None, ('win', 'row')), parts along dimension 1, may hold values from -6 to 6
- target: int32 [4096, 128], P(('win', 'row')), parts along dimension 0, may hold values 0 or 1
- kernel_taps: float32 [24, 2, 128, 128], replicated, may hold values from -0.046875 to 0.046875
- kernel_radii: int32 [24], replicated, may hold values from 16 to 64, as said below
- kernel_group: int32 [24], replicated, may hold values from 0 to 2, as said below
- kernel_weight: float32 [24], replicated, may hold values from 0.1 to 1
Outputs:
- resist: float32 [3, 4096, 128], P(None, ('win', 'row')), parts along dimension 1
- gradient: float32 [2, 4096, 128], P(None, ('win', 'row')), parts along dimension 1
The draws below stay inside these ranges and needn't reach their ends.
There are 2 independent parts, one for each index of `win`. The reference program is written for one: setup_inputs(seed, part) draws one part's arguments, and reference() takes and returns one part's arrays. A program takes and returns all parts, laid end to end along the dimension named above; an argument that names none is the same for every part. Nothing has to cross between parts.
Inputs may be any that keep to these rules, and one draw needn't show every extreme that they name: `kernel_radii`: every radius lies in 16 to 64; some kernel has radius exactly 64 and some exactly 16. `kernel_group`: every one of the 3 process conditions holds at least one kernel.
All inputs are finite; a program needn't handle non-finite values. No bound on the sum of `target` on one device may be relied on, other than what follows from the above.
Results may differ from the reference program's by a relative error of at most 0.0003.
Values sent between devices are 32-bit elements; how exact they have to be, the bound alone decides.
A program may use at most 128 MiB of HBM per device.

```python
import math
import jax
import jax.numpy as jnp
from jax import lax

COLS = 128
RMAX = 64
RMIN = 16
KERNELS = 24
GROUPS = 3
ROWS = 2048


def draw_kernel_radii(key, part):
    key = jax.random.fold_in(key, 11)
    first_key, second_key = jax.random.split(key)
    values = jax.random.randint(first_key, (KERNELS,), RMIN, RMAX + 1)
    order = jax.random.permutation(second_key, KERNELS)
    values = values.at[order[0]].set(RMAX)
    values = values.at[order[1]].set(RMIN)
    return values.astype(jnp.int32)


def draw_kernel_group(key, part):
    key = jax.random.fold_in(key, 23)
    first_key, second_key = jax.random.split(key)
    values = jax.random.randint(first_key, (KERNELS,), 0, GROUPS)
    order = jax.random.permutation(second_key, KERNELS)
    values = values.at[order[:GROUPS]].set(jnp.arange(GROUPS, dtype=jnp.int32))
    return values.astype(jnp.int32)


def with_ends(result, rng, smallest, top_value):
    longest = result.shape.index(max(result.shape))
    spots = []
    for shift in (0, 1):
        where = [jax.random.randint(jax.random.fold_in(rng, axis), (), 0, length) for axis, length in enumerate(result.shape)]
        where[longest] = (where[longest] + shift) % result.shape[longest]
        spots.append(tuple(where))
    return result.at[spots[0]].set(smallest).at[spots[1]].set(top_value)


def levels(rng, extent, shards, least, high):
    level, own = 1.0, jax.random.fold_in(rng, 6)
    for axis_at, shards_of in shards:
        steps = jnp.exp(jax.random.uniform(jax.random.fold_in(own, axis_at), (shards_of,), jnp.float32, least / len(shards), high / len(shards)))
        level = level * jnp.repeat(steps, extent[axis_at] // shards_of).reshape([-1 if axis == axis_at else 1 for axis in range(len(extent))])
    return level


def normal_values(key, shape, spread, bound, pieces=(), held_as=jnp.bfloat16):
    loudness = levels(key, shape, pieces, -0.22, 0.18) if pieces else 1.0
    drawn = jax.random.normal(key, shape, jnp.float32) * spread * loudness
    return jnp.minimum(jnp.maximum(drawn, -bound), bound).astype(held_as)


def setup_inputs(seed: int = 0, part: int = 0) -> dict:
    key_of = jax.random.split(jax.random.key(seed), 7)
    part_splits = jax.random.split(jax.random.fold_in(key_of[6], part), 7)
    mask_field = normal_values(part_splits[0], (2, ROWS, COLS), 1.0, 6.0, ((1, 16),), jnp.float32)
    target = with_ends((jax.random.randint(part_splits[1], (ROWS, COLS), 0, 2) < 1).astype(jnp.int32), jax.random.fold_in(part_splits[1], 1), 0, 1)
    kernel_taps = normal_values(key_of[2], (KERNELS, 2, 2 * RMAX, 2 * RMAX), (4 * RMAX * RMAX) ** -0.5, 0.046875, (), jnp.float32)
    kernel_radii = draw_kernel_radii(jax.random.fold_in(key_of[6], 71), part)
    kernel_group = draw_kernel_group(jax.random.fold_in(key_of[6], 71), part)
    kernel_weight = jnp.clip(jnp.exp(jax.random.uniform(key_of[5], (KERNELS,), jnp.float32, math.log(0.1), math.log(1.0))), 0.1, 1.0)
    return {"mask_field": mask_field, "target": target, "kernel_taps": kernel_taps, "kernel_radii": kernel_radii, "kernel_group": kernel_group, "kernel_weight": kernel_weight}


steepness = 1.0
threshold = 2.0

def kernel_spectrum(tap_real, tap_imag, radius, grid_rows, grid_cols):
    offsets = jnp.arange(2 * RMAX, dtype=jnp.int32) - RMAX
    inside = ((offsets >= -radius) & (offsets < radius)).astype(jnp.float32)
    kept_taps = inside[:, None] * inside[None, :]
    complex_taps = lax.complex(tap_real * kept_taps, tap_imag * kept_taps)
    placed = jnp.pad(complex_taps, ((0, grid_rows - 2 * RMAX), (0, grid_cols - 2 * RMAX)))
    placed = jnp.roll(placed, (-RMAX, -RMAX), axis=(0, 1))
    return jnp.fft.fft2(placed)

def convolve(mask_real, mask_imag, spectrum):
    total_rows = mask_real.shape[0]
    total_cols = mask_real.shape[1]
    grid = jnp.pad(lax.complex(mask_real, mask_imag), ((0, 2 * RMAX), (0, 2 * RMAX)))
    result_field = jnp.fft.ifft2(jnp.fft.fft2(grid) * spectrum)[:total_rows, :total_cols]
    return (jnp.real(result_field), jnp.imag(result_field))

def reference(mask_field, target, kernel_taps, kernel_radii, kernel_group, kernel_weight):
    total_rows = mask_field.shape[1]
    total_cols = mask_field.shape[2]
    grid_rows = total_rows + 2 * RMAX
    grid_cols = total_cols + 2 * RMAX
    onehot = (kernel_group[:, None] == jnp.arange(GROUPS, dtype=jnp.int32)[None, :]).astype(jnp.float32)
    mixing = kernel_weight[:, None] * onehot
    indices = jnp.arange(KERNELS, dtype=jnp.int32)

    def spectrum_of(index):
        return kernel_spectrum(kernel_taps[index, 0], kernel_taps[index, 1], kernel_radii[index], grid_rows, grid_cols)

    def forward_step(carry, index):
        field_real, field_imag = convolve(mask_field[0], mask_field[1], spectrum_of(index))
        power = field_real * field_real + field_imag * field_imag
        return (carry + mixing[index][:, None, None] * power[None], None)
    intensity, _ = lax.scan(forward_step, jnp.zeros((GROUPS, total_rows, total_cols), jnp.float32), indices)
    resist = jax.nn.sigmoid(steepness * (intensity - threshold))
    slopes = 2.0 * (resist - target.astype(jnp.float32)[None]) * resist * (1.0 - resist) * steepness

    def adjoint_step(carry, index):
        spectrum = spectrum_of(index)

        def linear(first_part, second_part):
            return convolve(first_part, second_part, spectrum)
        (field_real, field_imag), pullback = jax.vjp(linear, mask_field[0], mask_field[1])
        factor = 2.0 * lax.optimization_barrier(jnp.sum(mixing[index][:, None, None] * slopes, axis=0))
        grad_real, grad_imag = pullback((factor * field_real, factor * field_imag))
        return (carry + jnp.stack([grad_real, grad_imag]), None)
    gradient, _ = lax.scan(adjoint_step, jnp.zeros((2, total_rows, total_cols), jnp.float32), indices)
    return (resist, gradient)
```

```python
import numpy as np

import jax
import jax.numpy as jnp
from jax import lax
from jax.experimental import pallas as pl
from jax.experimental.pallas import tpu as pltpu
from jax.sharding import PartitionSpec as P

RMAX = 64
GROUPS = 3
STEEPNESS = 1.0
THRESHOLD = 2.0


def split_np(table):
    high = table.astype(jnp.bfloat16)
    low = (table - high.astype(np.float64)).astype(jnp.bfloat16)
    return high, low


def angles(points, grid):
    freqs = np.arange(grid // 2, dtype=np.int64)
    turns = (points.astype(np.int64)[:, None] * (2 * freqs[None, :] + 1)) % (2 * grid)
    return turns.astype(np.float64) * (np.pi / grid)


def tables(rows, cols):
    taps = 2 * RMAX
    grid_rows, grid_cols = rows + taps, cols + taps
    tap = np.arange(taps) - RMAX
    own, ext, col = np.arange(rows), np.arange(grid_rows) - RMAX, np.arange(cols)

    def right(points, grid):
        ang = angles(points, grid)
        high, low = split_np(np.concatenate([np.cos(ang), np.sin(ang)], 1))
        return np.stack([np.concatenate([high, high], 0), np.concatenate([low, low], 0)])

    def left(points, grid, deep):
        ang = angles(points, grid).T
        high, low = split_np(np.concatenate([np.cos(ang), np.sin(ang)], 0))
        if deep:
            high, low = np.concatenate([high, high], 1), np.concatenate([low, low], 1)
        return np.concatenate([high, low], 0)

    def back_left(points, grid):
        ang = angles(points, grid)
        high, low = split_np(np.concatenate([np.cos(ang), np.sin(ang)], 1) / grid)
        return np.concatenate([high, low], 0)

    def back_right(points, grid):
        ang = angles(points, grid).T
        high, low = split_np(np.concatenate([np.cos(ang), np.sin(ang)], 0) / grid)
        return np.concatenate([high, low], 1)

    return (
        right(tap, grid_cols),
        right(col, grid_cols),
        left(tap, grid_rows, True),
        left(own, grid_rows, True),
        left(ext, grid_rows, False),
        back_left(own, grid_rows),
        back_left(ext, grid_rows),
        back_right(col, grid_cols),
    )


def dot(a, b):
    return lax.dot_general(a, b, (((1,), (0,)), ((), ())), preferred_element_type=jnp.float32)


def split(value):
    high = value.astype(jnp.bfloat16)
    low = (value - high.astype(jnp.float32)).astype(jnp.bfloat16)
    return high, low


def col_transform(pair, table):
    high, low = split(pair)
    data = jnp.concatenate([high, low], axis=1)
    return dot(data, table[0]) + dot(data, table[1])


def fold(value):
    half = value.shape[0] // 2
    return value[:half] + value[half:]


def row_transform(value, table):
    high, low = split(value)
    return fold(dot(table, jnp.concatenate([high, low], axis=0)))


def row_transform_wide(value, table):
    high, low = split(value)
    return fold(dot(table, high)) + dot(table[: table.shape[0] // 2], low)


def quadrants(real, imag):
    g, f = real.shape[0] // 2, real.shape[1] // 2

    def parts(v):
        cp, cq, sp, sq = v[:g, :f], v[:g, f:], v[g:, :f], v[g:, f:]
        return cp - sq, sp + cq, cp + sq, sp - cq

    e1r, e2r, e3r, e4r = parts(real)
    e1i, e2i, e3i, e4i = parts(imag)
    return (
        (e1r + e2i, e1i - e2r),
        (e1r - e2i, e1i + e2r),
        (e3r + e4i, e3i - e4r),
        (e3r - e4i, e3i + e4r),
    )


def inverse(quads, row_table, col_table):
    (pr, pi), (mr, mi), (qr, qi), (nr, ni) = quads
    sr, dr, tr, er = pr + mr, pr - mr, qr + nr, qr - nr
    si, di, ti, ei = pi + mi, pi - mi, qi + ni, qi - ni

    def stack(a, b, c, d):
        return jnp.concatenate(
            [jnp.concatenate([a, b], axis=1), jnp.concatenate([c, d], axis=1)], axis=0
        )

    real = stack(sr + tr, ei - di, -di - ei, tr - sr)
    imag = stack(si + ti, dr - er, dr + er, ti - si)
    half = jnp.concatenate(
        [row_transform_wide(real, row_table), row_transform_wide(imag, row_table)], axis=0
    )
    high, low = split(half)
    both = fold(dot(jnp.concatenate([high, low], axis=0), col_table))
    width = both.shape[1] // 2
    return both[:, :width] + both[:, width:]


def body(
    radii_ref,
    group_ref,
    weight_ref,
    taps_ref,
    mask_ref,
    target_ref,
    tap_col,
    own_col,
    tap_row,
    own_row,
    ext_row,
    back_own,
    back_ext,
    back_col,
    resist_ref,
    adjoint_ref,
    spec,
    fields,
    mask_spec,
    total,
):
    kernels = taps_ref.shape[0]
    taps = taps_ref.shape[2]
    rows, cols = target_ref.shape

    def spectrum(k, carry):
        radius = radii_ref[k]
        a = lax.broadcasted_iota(jnp.int32, (taps, taps), 0) - RMAX
        b = lax.broadcasted_iota(jnp.int32, (taps, taps), 1) - RMAX
        inside = (a >= -radius) & (a < radius) & (b >= -radius) & (b < radius)
        pair = jnp.concatenate(
            [jnp.where(inside, taps_ref[k, 0], 0.0), jnp.where(inside, taps_ref[k, 1], 0.0)], axis=0
        )
        half = col_transform(pair, tap_col)
        real = row_transform(half[:taps], tap_row[...])
        imag = row_transform(half[taps:], tap_row[...])
        for q, (re, im) in enumerate(quadrants(real, imag)):
            spec[k, 2 * q] = re
            spec[k, 2 * q + 1] = im
        return carry

    lax.fori_loop(0, kernels, spectrum, 0)

    ext = mask_ref.shape[1]
    half = col_transform(jnp.concatenate([mask_ref[0], mask_ref[1]], axis=0), own_col)
    real = row_transform_wide(half[:ext], ext_row[...])
    imag = row_transform_wide(half[ext:], ext_row[...])
    for q, (re, im) in enumerate(quadrants(real, imag)):
        mask_spec[2 * q] = re
        mask_spec[2 * q + 1] = im

    resist_ref[...] = jnp.zeros_like(resist_ref)

    def mixed(k, g):
        return jnp.where(group_ref[k] == g, weight_ref[k], 0.0)

    def forward(k, carry):
        quads = []
        for q in range(4):
            xr, xi = spec[k, 2 * q], spec[k, 2 * q + 1]
            mr, mi = mask_spec[2 * q], mask_spec[2 * q + 1]
            quads.append((xr * mr - xi * mi, xr * mi + xi * mr))
        field = inverse(quads, back_own[...], back_col[...])
        fields[k] = field
        power = field[:rows] * field[:rows] + field[rows:] * field[rows:]
        for g in range(GROUPS):
            resist_ref[g] += mixed(k, g) * power
        return carry

    lax.fori_loop(0, kernels, forward, 0)

    target = target_ref[...].astype(jnp.float32)
    slopes = []
    for g in range(GROUPS):
        resist = jax.nn.sigmoid(STEEPNESS * (resist_ref[g] - THRESHOLD))
        resist_ref[g] = resist
        total[g] = 2.0 * (resist - target) * resist * (1.0 - resist) * STEEPNESS
    for q in range(8):
        mask_spec[q] = jnp.zeros_like(mask_spec[q])

    def backward(k, carry):
        factor = sum(2.0 * mixed(k, g) * total[g] for g in range(GROUPS))
        field = fields[k]
        cot = jnp.concatenate([factor * field[:rows], factor * field[rows:]], axis=0)
        half = col_transform(cot, own_col)
        real = row_transform(half[:rows], own_row[...])
        imag = row_transform(half[rows:], own_row[...])
        for q, (wr, wi) in enumerate(quadrants(real, imag)):
            xr, xi = spec[k, 2 * q], spec[k, 2 * q + 1]
            mask_spec[2 * q] += xr * wr + xi * wi
            mask_spec[2 * q + 1] += xr * wi - xi * wr
        return carry

    lax.fori_loop(0, kernels, backward, 0)
    quads = [(mask_spec[2 * q], mask_spec[2 * q + 1]) for q in range(4)]
    adjoint = inverse(quads, back_ext[...], back_col[...])
    adjoint_ref[0] = adjoint[:ext]
    adjoint_ref[1] = adjoint[ext:]


def padded(cells, width):
    count = lax.axis_size("row")
    head, tail = cells[:, :width], cells[:, cells.shape[1] - width :]
    above = lax.ppermute(tail, "row", [(i, i + 1) for i in range(count - 1)])
    below = lax.ppermute(head, "row", [(i + 1, i) for i in range(count - 1)])
    return jnp.concatenate([above, cells, below], axis=1)


def on_device(mask_field, target, kernel_taps, kernel_radii, kernel_group, kernel_weight):
    rows, cols = target.shape
    kernels = kernel_taps.shape[0]
    grid_rows, grid_cols = rows + 2 * RMAX, cols + 2 * RMAX
    consts = [jnp.asarray(t) for t in tables(rows, cols)]
    extended = padded(mask_field, RMAX)
    vmem = pl.BlockSpec(memory_space=pltpu.VMEM)
    smem = pl.BlockSpec(memory_space=pltpu.SMEM)
    plane = (grid_rows // 2, grid_cols // 2)
    resist, adjoint = pl.pallas_call(
        body,
        out_shape=(
            jax.ShapeDtypeStruct((GROUPS, rows, cols), jnp.float32),
            jax.ShapeDtypeStruct((2, grid_rows, cols), jnp.float32),
        ),
        in_specs=[smem] * 3 + [vmem] * (3 + len(consts)),
        out_specs=(vmem, vmem),
        scratch_shapes=[
            pltpu.VMEM((kernels, 8) + plane, jnp.float32),
            pltpu.VMEM((kernels, 2 * rows, cols), jnp.float32),
            pltpu.VMEM((8,) + plane, jnp.float32),
            pltpu.VMEM((GROUPS, rows, cols), jnp.float32),
        ],
        compiler_params=pltpu.CompilerParams(vmem_limit_bytes=48 * 1024 * 1024),
        name="litho",
    )(kernel_radii, kernel_group, kernel_weight, kernel_taps, extended, target, *consts)
    own = adjoint[:, RMAX : RMAX + rows]
    count = lax.axis_size("row")
    below = lax.ppermute(adjoint[:, :RMAX], "row", [(i + 1, i) for i in range(count - 1)])
    above = lax.ppermute(adjoint[:, RMAX + rows :], "row", [(i, i + 1) for i in range(count - 1)])
    rest = rows - RMAX
    gradient = (
        own
        + jnp.pad(above, ((0, 0), (0, rest), (0, 0)))
        + jnp.pad(below, ((0, 0), (rest, 0), (0, 0)))
    )
    return resist, gradient


def solution(mesh):
    in_specs = (P(None, ("win", "row"), None), P(("win", "row"), None), P(), P(), P(), P())
    out_specs = (P(None, ("win", "row"), None), P(None, ("win", "row"), None))
    return jax.shard_map(
        on_device, mesh=mesh, in_specs=in_specs, out_specs=out_specs, check_vma=False
    )
```

```python
import numpy as np

import jax
import jax.numpy as jnp
from jax import lax
from jax.experimental import pallas as pl
from jax.experimental.pallas import tpu as pltpu
from jax.sharding import PartitionSpec as P

RMAX = 64
GROUPS = 3
STEEPNESS = 1.0
THRESHOLD = 2.0
UNROLL = (1, 1, 1)
MESH = pl.DeviceIdType.MESH


def split_np(table):
    high = table.astype(jnp.bfloat16)
    low = (table - high.astype(np.float64)).astype(jnp.bfloat16)
    return high, low


def angles(points, grid):
    freqs = np.arange(grid // 2, dtype=np.int64)
    turns = (points.astype(np.int64)[:, None] * (2 * freqs[None, :] + 1)) % (2 * grid)
    return turns.astype(np.float64) * (np.pi / grid)


def tap_like(count):
    return np.arange(count) - RMAX


def tables(rows, cols):
    taps = 2 * RMAX
    grid_rows, grid_cols = rows + taps, cols + taps
    tap = np.arange(taps) - RMAX
    own, ext, col = tap_like(rows), np.arange(grid_rows) - 2 * RMAX, tap_like(cols)

    def right(points, grid):
        ang = angles(points, grid)
        high, low = split_np(np.concatenate([np.cos(ang), np.sin(ang)], 1))
        return np.stack([np.concatenate([high, high], 0), np.concatenate([low, low], 0)])

    def left(points, grid, deep):
        ang = angles(points, grid).T
        high, low = split_np(np.concatenate([np.cos(ang), np.sin(ang)], 0))
        if deep:
            high, low = np.concatenate([high, high], 1), np.concatenate([low, low], 1)
        return np.concatenate([high, low], 0)

    def back_left(points, grid):
        ang = angles(points, grid)
        high, low = split_np(np.concatenate([np.cos(ang), np.sin(ang)], 1) / grid)
        return np.concatenate([high, low], 0)

    def back_right(points, grid):
        ang = angles(points, grid).T
        high, low = split_np(np.concatenate([np.cos(ang), np.sin(ang)], 0) / grid)
        return np.concatenate([high, low], 1)

    return (
        right(tap, grid_cols),
        right(col, grid_cols),
        left(tap, grid_rows, True),
        left(own, grid_rows, True),
        left(ext, grid_rows, False),
        back_left(own, grid_rows),
        back_left(ext, grid_rows),
        back_right(col, grid_cols),
    )


def dot(a, b):
    return lax.dot_general(a, b, (((1,), (0,)), ((), ())), preferred_element_type=jnp.float32)


def split(value):
    high = value.astype(jnp.bfloat16)
    low = (value - high.astype(jnp.float32)).astype(jnp.bfloat16)
    return high, low


def col_transform(pair, table):
    high, low = split(pair)
    data = jnp.concatenate([high, low], axis=1)
    return dot(data, table[0]) + dot(data, table[1])


def fold(value):
    half = value.shape[0] // 2
    return value[:half] + value[half:]


def row_transform(value, table):
    high, low = split(value)
    return fold(dot(table, jnp.concatenate([high, low], axis=0)))


def row_transform_wide(value, table):
    high, low = split(value)
    return fold(dot(table, high)) + dot(table[: table.shape[0] // 2], low)


def quadrants(real, imag):
    g, f = real.shape[0] // 2, real.shape[1] // 2

    def parts(v):
        cp, cq, sp, sq = v[:g, :f], v[:g, f:], v[g:, :f], v[g:, f:]
        return cp - sq, sp + cq, cp + sq, sp - cq

    e1r, e2r, e3r, e4r = parts(real)
    e1i, e2i, e3i, e4i = parts(imag)
    return (
        (e1r + e2i, e1i - e2r),
        (e1r - e2i, e1i + e2r),
        (e3r + e4i, e3i - e4r),
        (e3r - e4i, e3i + e4r),
    )


def inverse(quads, row_table, col_table):
    (pr, pi), (mr, mi), (qr, qi), (nr, ni) = quads
    sr, dr, tr, er = pr + mr, pr - mr, qr + nr, qr - nr
    si, di, ti, ei = pi + mi, pi - mi, qi + ni, qi - ni

    def stack(a, b, c, d):
        return jnp.concatenate(
            [jnp.concatenate([a, b], axis=1), jnp.concatenate([c, d], axis=1)], axis=0
        )

    real = stack(sr + tr, ei - di, -di - ei, tr - sr)
    imag = stack(si + ti, dr - er, dr + er, ti - si)
    half = jnp.concatenate(
        [row_transform_wide(real, row_table), row_transform_wide(imag, row_table)], axis=0
    )
    high, low = split(half)
    both = fold(dot(jnp.concatenate([high, low], axis=0), col_table))
    width = both.shape[1] // 2
    return both[:, :width] + both[:, width:]


def body(
    radii_ref,
    group_ref,
    weight_ref,
    taps_hbm,
    mask_hbm,
    target_hbm,
    *refs,
):
    table_hbm, refs = refs[:8], refs[8:]
    resist_ref, grad_ref = refs[:2]
    spec, fields, acc, slopes, taps_ref, ext_ref, target_ref, adj, rims = refs[2:11]
    table_ref, refs = refs[11:19], refs[19:]
    tap_sem, load_sem, send_sem, recv_sem = refs
    tap_col, own_col, tap_row, own_row, ext_row, back_own, back_ext, back_col = table_ref
    kernels, _, taps, _ = taps_hbm.shape
    rows, cols = target_hbm.shape
    me, count = lax.axis_index("row"), lax.axis_size("row")
    has_prev, has_next = me > 0, me < count - 1
    prev_id = {"row": lax.rem(me + count - 1, count)}
    next_id = {"row": lax.rem(me + 1, count)}

    def load(src, dst, slot):
        return pltpu.make_async_copy(src, dst, load_sem.at[slot])

    def tap_load(k):
        return pltpu.make_async_copy(taps_hbm.at[k], taps_ref.at[k], tap_sem.at[k])

    loads = [load(src, dst, i) for i, (src, dst) in enumerate(zip(table_hbm, table_ref))]
    load_mask = load(mask_hbm, ext_ref.at[:, pl.ds(RMAX, rows)], 8)
    load_target = load(target_hbm, target_ref, 9)
    loads[0].start()
    loads[2].start()

    def start_tap(k, carry):
        tap_load(k).start()
        return carry

    lax.fori_loop(0, kernels, start_tap, 0)
    load_mask.start()
    load_target.start()
    for i in (1, 3, 4, 5, 6, 7):
        loads[i].start()

    barrier = pltpu.get_barrier_semaphore()

    @pl.when(has_prev)
    def _():
        pl.semaphore_signal(barrier, inc=1, device_id=prev_id, device_id_type=MESH)

    @pl.when(has_next)
    def _():
        pl.semaphore_signal(barrier, inc=1, device_id=next_id, device_id_type=MESH)

    pl.semaphore_wait(barrier, has_prev.astype(jnp.int32) + has_next.astype(jnp.int32))

    def exchange(first, src_up, dst_up, src_down, dst_down):
        down = pltpu.make_async_remote_copy(
            src_ref=src_down,
            dst_ref=dst_down,
            send_sem=send_sem.at[first],
            recv_sem=recv_sem.at[first],
            device_id=next_id,
            device_id_type=MESH,
        )
        up = pltpu.make_async_remote_copy(
            src_ref=src_up,
            dst_ref=dst_up,
            send_sem=send_sem.at[first + 1],
            recv_sem=recv_sem.at[first + 1],
            device_id=prev_id,
            device_id_type=MESH,
        )
        return up, down

    def start_both(pair):
        up, down = pair

        @pl.when(has_next)
        def _():
            down.start()

        @pl.when(has_prev)
        def _():
            up.start()

    def wait_both(pair):
        up, down = pair

        @pl.when(has_prev)
        def _():
            up.wait_send()
            down.wait_recv()

        @pl.when(has_next)
        def _():
            down.wait_send()
            up.wait_recv()

    halo = exchange(
        0,
        mask_hbm.at[:, pl.ds(0, RMAX)],
        ext_ref.at[:, pl.ds(RMAX + rows, RMAX)],
        mask_hbm.at[:, pl.ds(rows - RMAX, RMAX)],
        ext_ref.at[:, pl.ds(0, RMAX)],
    )
    start_both(halo)

    @pl.when(jnp.logical_not(has_prev))
    def _():
        ext_ref[:, :RMAX] = jnp.zeros_like(ext_ref[:, :RMAX])
        rims[0] = jnp.zeros_like(rims[0])

    @pl.when(jnp.logical_not(has_next))
    def _():
        ext_ref[:, RMAX + rows :] = jnp.zeros_like(ext_ref[:, RMAX + rows :])
        rims[1] = jnp.zeros_like(rims[1])

    loads[0].wait()
    loads[2].wait()

    def spectrum(k, carry):
        tap_load(k).wait()
        radius = radii_ref[k]
        a = lax.broadcasted_iota(jnp.int32, (taps, taps), 0) - RMAX
        b = lax.broadcasted_iota(jnp.int32, (taps, taps), 1) - RMAX
        inside = (a >= -radius) & (a < radius) & (b >= -radius) & (b < radius)
        pair = jnp.concatenate(
            [jnp.where(inside, taps_ref[k, 0], 0.0), jnp.where(inside, taps_ref[k, 1], 0.0)], axis=0
        )
        half = col_transform(pair, tap_col)
        real = row_transform(half[:taps], tap_row[...])
        imag = row_transform(half[taps:], tap_row[...])
        for q, (re, im) in enumerate(quadrants(real, imag)):
            spec[k, 2 * q] = re
            spec[k, 2 * q + 1] = im
        return carry

    lax.fori_loop(0, kernels, spectrum, 0, unroll=UNROLL[0])

    load_mask.wait()
    load_target.wait()
    for i in (1, 3, 4, 5, 6, 7):
        loads[i].wait()
    wait_both(halo)

    ext = ext_ref.shape[1]
    half = col_transform(jnp.concatenate([ext_ref[0], ext_ref[1]], axis=0), own_col)
    real = row_transform_wide(half[:ext], ext_row[...])
    imag = row_transform_wide(half[ext:], ext_row[...])
    for q, (re, im) in enumerate(quadrants(real, imag)):
        acc[2 * q] = re
        acc[2 * q + 1] = im

    resist_ref[...] = jnp.zeros_like(resist_ref)

    def mixed(k, g):
        return jnp.where(group_ref[k] == g, weight_ref[k], 0.0)

    def forward(k, carry):
        quads = []
        for q in range(4):
            xr, xi = spec[k, 2 * q], spec[k, 2 * q + 1]
            mr, mi = acc[2 * q], acc[2 * q + 1]
            quads.append((xr * mr - xi * mi, xr * mi + xi * mr))
        field = inverse(quads, back_own[...], back_col[...])
        fields[k] = field
        power = field[:rows] * field[:rows] + field[rows:] * field[rows:]
        for g in range(GROUPS):
            resist_ref[g] += mixed(k, g) * power
        return carry

    lax.fori_loop(0, kernels, forward, 0, unroll=UNROLL[1])

    target = target_ref[...].astype(jnp.float32)
    for g in range(GROUPS):
        resist = jax.nn.sigmoid(STEEPNESS * (resist_ref[g] - THRESHOLD))
        resist_ref[g] = resist
        slopes[g] = 2.0 * (resist - target) * resist * (1.0 - resist) * STEEPNESS
    acc[...] = jnp.zeros_like(acc)

    def backward(k, carry):
        factor = sum(2.0 * mixed(k, g) * slopes[g] for g in range(GROUPS))
        field = fields[k]
        cot = jnp.concatenate([factor * field[:rows], factor * field[rows:]], axis=0)
        half = col_transform(cot, own_col)
        real = row_transform(half[:rows], own_row[...])
        imag = row_transform(half[rows:], own_row[...])
        for q, (wr, wi) in enumerate(quadrants(real, imag)):
            xr, xi = spec[k, 2 * q], spec[k, 2 * q + 1]
            acc[2 * q] += xr * wr + xi * wi
            acc[2 * q + 1] += xr * wi - xi * wr
        return carry

    lax.fori_loop(0, kernels, backward, 0, unroll=UNROLL[2])
    quads = [(acc[2 * q], acc[2 * q + 1]) for q in range(4)]
    adjoint = inverse(quads, back_ext[...], back_col[...])
    adj[0] = adjoint[:ext]
    adj[1] = adjoint[ext:]
    back = exchange(
        2,
        adj.at[:, pl.ds(0, RMAX)],
        rims.at[1],
        adj.at[:, pl.ds(RMAX + rows, RMAX)],
        rims.at[0],
    )
    start_both(back)
    grad_ref[...] = adj[:, RMAX : RMAX + rows]
    wait_both(back)
    grad_ref[:, :RMAX] += rims[0]
    grad_ref[:, rows - RMAX :] += rims[1]


def on_device(mask_field, target, kernel_taps, kernel_radii, kernel_group, kernel_weight):
    rows, cols = target.shape
    kernels, _, taps, _ = kernel_taps.shape
    grid_rows, grid_cols = rows + taps, cols + taps
    consts = [jnp.asarray(t) for t in tables(rows, cols)]
    vmem = pl.BlockSpec(memory_space=pltpu.VMEM)
    smem = pl.BlockSpec(memory_space=pltpu.SMEM)
    hbm = pl.BlockSpec(memory_space=pltpu.HBM)
    plane = (grid_rows // 2, grid_cols // 2)
    return pl.pallas_call(
        body,
        out_shape=(
            jax.ShapeDtypeStruct((GROUPS, rows, cols), jnp.float32),
            jax.ShapeDtypeStruct((2, rows, cols), jnp.float32),
        ),
        in_specs=[smem] * 3 + [hbm] * (3 + len(consts)),
        out_specs=(vmem, vmem),
        scratch_shapes=[
            pltpu.VMEM((kernels, 8) + plane, jnp.float32),
            pltpu.VMEM((kernels, 2 * rows, cols), jnp.float32),
            pltpu.VMEM((8,) + plane, jnp.float32),
            pltpu.VMEM((GROUPS, rows, cols), jnp.float32),
            pltpu.VMEM(kernel_taps.shape, jnp.float32),
            pltpu.VMEM((2, grid_rows, cols), jnp.float32),
            pltpu.VMEM((rows, cols), jnp.int32),
            pltpu.VMEM((2, grid_rows, cols), jnp.float32),
            pltpu.VMEM((2, 2, RMAX, cols), jnp.float32),
        ]
        + [pltpu.VMEM(t.shape, t.dtype) for t in consts]
        + [
            pltpu.SemaphoreType.DMA((kernels,)),
            pltpu.SemaphoreType.DMA((10,)),
            pltpu.SemaphoreType.DMA((4,)),
            pltpu.SemaphoreType.DMA((4,)),
        ],
        compiler_params=pltpu.CompilerParams(
            vmem_limit_bytes=56 * 1024 * 1024, collective_id=0, has_side_effects=True
        ),
        name="litho",
    )(kernel_radii, kernel_group, kernel_weight, kernel_taps, mask_field, target, *consts)


def solution(mesh):
    in_specs = (P(None, ("win", "row"), None), P(("win", "row"), None), P(), P(), P(), P())
    out_specs = (P(None, ("win", "row"), None), P(None, ("win", "row"), None))
    return jax.shard_map(
        on_device, mesh=mesh, in_specs=in_specs, out_specs=out_specs, check_vma=False
    )
```

```python
import numpy as np

import jax
import jax.numpy as jnp
from jax import lax
from jax.experimental import pallas as pl
from jax.experimental.pallas import tpu as pltpu
from jax.sharding import PartitionSpec as P

RMAX = 64
GROUPS = 3
STEEPNESS = 1.0
THRESHOLD = 2.0
UNROLL = (4, 6, 6)
MESH = pl.DeviceIdType.MESH


def split_np(table):
    high = table.astype(jnp.bfloat16)
    low = (table - high.astype(np.float64)).astype(jnp.bfloat16)
    return high, low


def angles(points, grid):
    freqs = np.arange(grid // 2, dtype=np.int64)
    turns = (points.astype(np.int64)[:, None] * (2 * freqs[None, :] + 1)) % (2 * grid)
    return turns.astype(np.float64) * (np.pi / grid)


def tap_like(count):
    return np.arange(count) - RMAX


def tables(rows, cols):
    taps = 2 * RMAX
    grid_rows, grid_cols = rows + taps, cols + taps
    tap = np.arange(taps) - RMAX
    own, ext, col = tap_like(rows), np.arange(grid_rows) - 2 * RMAX, tap_like(cols)

    def right(points, grid):
        ang = angles(points, grid)
        high, low = split_np(np.concatenate([np.cos(ang), np.sin(ang)], 1))
        return np.stack([np.concatenate([high, high], 0), np.concatenate([low, low], 0)])

    def left(points, grid, deep):
        ang = angles(points, grid).T
        high, low = split_np(np.concatenate([np.cos(ang), np.sin(ang)], 0))
        if deep:
            high, low = np.concatenate([high, high], 1), np.concatenate([low, low], 1)
        return np.concatenate([high, low], 0)

    def back_left(points, grid):
        ang = angles(points, grid)
        high, low = split_np(np.concatenate([np.cos(ang), np.sin(ang)], 1) / grid)
        return np.concatenate([high, low], 0)

    def back_right(points, grid):
        ang = angles(points, grid).T
        high, low = split_np(np.concatenate([np.cos(ang), np.sin(ang)], 0) / grid)
        return np.concatenate([high, low], 1)

    return (
        right(tap, grid_cols),
        right(col, grid_cols),
        left(tap, grid_rows, True),
        left(own, grid_rows, True),
        left(ext, grid_rows, False),
        back_left(own, grid_rows),
        back_left(ext, grid_rows),
        back_right(col, grid_cols),
    )


def resist_of(intensity):
    return jax.nn.sigmoid(STEEPNESS * (intensity - THRESHOLD))


def dot(a, b):
    return lax.dot_general(a, b, (((1,), (0,)), ((), ())), preferred_element_type=jnp.float32)


def split(value):
    high = value.astype(jnp.bfloat16)
    low = (value - high.astype(jnp.float32)).astype(jnp.bfloat16)
    return high, low


def col_transform(pair, table):
    high, low = split(pair)
    data = jnp.concatenate([high, low], axis=1)
    return dot(data, table[0]) + dot(data, table[1])


def fold(value):
    half = value.shape[0] // 2
    return value[:half] + value[half:]


def row_transform(value, table):
    high, low = split(value)
    return fold(dot(table, jnp.concatenate([high, low], axis=0)))


def row_transform_wide(value, table):
    high, low = split(value)
    return fold(dot(table, high)) + dot(table[: table.shape[0] // 2], low)


def quadrants(real, imag):
    g, f = real.shape[0] // 2, real.shape[1] // 2

    def parts(v):
        cp, cq, sp, sq = v[:g, :f], v[:g, f:], v[g:, :f], v[g:, f:]
        return cp - sq, sp + cq, cp + sq, sp - cq

    e1r, e2r, e3r, e4r = parts(real)
    e1i, e2i, e3i, e4i = parts(imag)
    return (
        (e1r + e2i, e1i - e2r),
        (e1r - e2i, e1i + e2r),
        (e3r + e4i, e3i - e4r),
        (e3r - e4i, e3i + e4r),
    )


def inverse(quads, row_table, col_table):
    (pr, pi), (mr, mi), (qr, qi), (nr, ni) = quads
    sr, dr, tr, er = pr + mr, pr - mr, qr + nr, qr - nr
    si, di, ti, ei = pi + mi, pi - mi, qi + ni, qi - ni

    def stack(a, b, c, d):
        return jnp.concatenate(
            [jnp.concatenate([a, b], axis=1), jnp.concatenate([c, d], axis=1)], axis=0
        )

    real = stack(sr + tr, ei - di, -di - ei, tr - sr)
    imag = stack(si + ti, dr - er, dr + er, ti - si)
    half = jnp.concatenate(
        [row_transform_wide(real, row_table), row_transform_wide(imag, row_table)], axis=0
    )
    high, low = split(half)
    both = fold(dot(jnp.concatenate([high, low], axis=0), col_table))
    width = both.shape[1] // 2
    return both[:, :width] + both[:, width:]


def body(
    radii_ref,
    group_ref,
    weight_ref,
    taps_hbm,
    mask_hbm,
    target_hbm,
    *refs,
):
    table_hbm, refs = refs[:8], refs[8:]
    power_ref, own_ref, rim_ref = refs[:3]
    spec, fields, acc, slopes, taps_ref, ext_ref, target_ref, adj, rims = refs[3:12]
    table_ref, refs = refs[12:20], refs[20:]
    tap_sem, load_sem, send_sem, recv_sem = refs
    tap_col, own_col, tap_row, own_row, ext_row, back_own, back_ext, back_col = table_ref
    kernels, _, taps, _ = taps_hbm.shape
    rows, cols = target_hbm.shape
    me, count = lax.axis_index("row"), lax.axis_size("row")
    has_prev, has_next = me > 0, me < count - 1
    prev_id = {"row": lax.rem(me + count - 1, count)}
    next_id = {"row": lax.rem(me + 1, count)}

    def load(src, dst, slot):
        return pltpu.make_async_copy(src, dst, load_sem.at[slot])

    def tap_load(k):
        return pltpu.make_async_copy(taps_hbm.at[k], taps_ref.at[k], tap_sem.at[k])

    loads = [load(src, dst, i) for i, (src, dst) in enumerate(zip(table_hbm, table_ref))]
    load_mask = load(mask_hbm, ext_ref.at[:, pl.ds(RMAX, rows)], 8)
    load_target = load(target_hbm, target_ref, 9)
    loads[0].start()
    loads[2].start()

    def start_tap(k, carry):
        tap_load(k).start()
        return carry

    lax.fori_loop(0, kernels, start_tap, 0)
    load_mask.start()
    load_target.start()
    for i in (1, 3, 4, 5, 6, 7):
        loads[i].start()

    barrier = pltpu.get_barrier_semaphore()

    @pl.when(has_prev)
    def _():
        pl.semaphore_signal(barrier, inc=1, device_id=prev_id, device_id_type=MESH)

    @pl.when(has_next)
    def _():
        pl.semaphore_signal(barrier, inc=1, device_id=next_id, device_id_type=MESH)

    pl.semaphore_wait(barrier, has_prev.astype(jnp.int32) + has_next.astype(jnp.int32))

    def exchange(first, src_up, dst_up, src_down, dst_down):
        down = pltpu.make_async_remote_copy(
            src_ref=src_down,
            dst_ref=dst_down,
            send_sem=send_sem.at[first],
            recv_sem=recv_sem.at[first],
            device_id=next_id,
            device_id_type=MESH,
        )
        up = pltpu.make_async_remote_copy(
            src_ref=src_up,
            dst_ref=dst_up,
            send_sem=send_sem.at[first + 1],
            recv_sem=recv_sem.at[first + 1],
            device_id=prev_id,
            device_id_type=MESH,
        )
        return up, down

    def start_both(pair):
        up, down = pair

        @pl.when(has_next)
        def _():
            down.start()

        @pl.when(has_prev)
        def _():
            up.start()

    def wait_both(pair):
        up, down = pair

        @pl.when(has_prev)
        def _():
            up.wait_send()
            down.wait_recv()

        @pl.when(has_next)
        def _():
            down.wait_send()
            up.wait_recv()

    halo = exchange(
        0,
        mask_hbm.at[:, pl.ds(0, RMAX)],
        ext_ref.at[:, pl.ds(RMAX + rows, RMAX)],
        mask_hbm.at[:, pl.ds(rows - RMAX, RMAX)],
        ext_ref.at[:, pl.ds(0, RMAX)],
    )
    start_both(halo)

    @pl.when(jnp.logical_not(has_prev))
    def _():
        ext_ref[:, :RMAX] = jnp.zeros_like(ext_ref[:, :RMAX])
        rims[0] = jnp.zeros_like(rims[0])

    @pl.when(jnp.logical_not(has_next))
    def _():
        ext_ref[:, RMAX + rows :] = jnp.zeros_like(ext_ref[:, RMAX + rows :])
        rims[1] = jnp.zeros_like(rims[1])

    loads[0].wait()
    loads[2].wait()

    def spectrum(k, carry):
        tap_load(k).wait()
        radius = radii_ref[k]
        a = lax.broadcasted_iota(jnp.int32, (taps, taps), 0) - RMAX
        b = lax.broadcasted_iota(jnp.int32, (taps, taps), 1) - RMAX
        inside = (a >= -radius) & (a < radius) & (b >= -radius) & (b < radius)
        pair = jnp.concatenate(
            [jnp.where(inside, taps_ref[k, 0], 0.0), jnp.where(inside, taps_ref[k, 1], 0.0)], axis=0
        )
        half = col_transform(pair, tap_col)
        real = row_transform(half[:taps], tap_row[...])
        imag = row_transform(half[taps:], tap_row[...])
        for q, (re, im) in enumerate(quadrants(real, imag)):
            spec[k, 2 * q] = re
            spec[k, 2 * q + 1] = im
        return carry

    lax.fori_loop(0, kernels, spectrum, 0, unroll=UNROLL[0])

    load_mask.wait()
    load_target.wait()
    for i in (1, 3, 4, 5, 6, 7):
        loads[i].wait()
    wait_both(halo)

    ext = ext_ref.shape[1]
    half = col_transform(jnp.concatenate([ext_ref[0], ext_ref[1]], axis=0), own_col)
    real = row_transform_wide(half[:ext], ext_row[...])
    imag = row_transform_wide(half[ext:], ext_row[...])
    for q, (re, im) in enumerate(quadrants(real, imag)):
        acc[2 * q] = re
        acc[2 * q + 1] = im

    power_ref[...] = jnp.zeros_like(power_ref)

    def mixed(k, g):
        return jnp.where(group_ref[k] == g, weight_ref[k], 0.0)

    def forward(k, carry):
        quads = []
        for q in range(4):
            xr, xi = spec[k, 2 * q], spec[k, 2 * q + 1]
            mr, mi = acc[2 * q], acc[2 * q + 1]
            quads.append((xr * mr - xi * mi, xr * mi + xi * mr))
        field = inverse(quads, back_own[...], back_col[...])
        fields[k] = field
        power = field[:rows] * field[:rows] + field[rows:] * field[rows:]
        for g in range(GROUPS):
            power_ref[g] += mixed(k, g) * power
        return carry

    lax.fori_loop(0, kernels, forward, 0, unroll=UNROLL[1])

    target = target_ref[...].astype(jnp.float32)
    for g in range(GROUPS):
        resist = resist_of(power_ref[g])
        slopes[g] = 2.0 * (resist - target) * resist * (1.0 - resist) * STEEPNESS
    acc[...] = jnp.zeros_like(acc)

    def backward(k, carry):
        factor = sum(2.0 * mixed(k, g) * slopes[g] for g in range(GROUPS))
        field = fields[k]
        cot = jnp.concatenate([factor * field[:rows], factor * field[rows:]], axis=0)
        half = col_transform(cot, own_col)
        real = row_transform(half[:rows], own_row[...])
        imag = row_transform(half[rows:], own_row[...])
        for q, (wr, wi) in enumerate(quadrants(real, imag)):
            xr, xi = spec[k, 2 * q], spec[k, 2 * q + 1]
            acc[2 * q] += xr * wr + xi * wi
            acc[2 * q + 1] += xr * wi - xi * wr
        return carry

    lax.fori_loop(0, kernels, backward, 0, unroll=UNROLL[2])
    quads = [(acc[2 * q], acc[2 * q + 1]) for q in range(4)]
    adjoint = inverse(quads, back_ext[...], back_col[...])
    adj[0] = adjoint[:ext]
    adj[1] = adjoint[ext:]
    back = exchange(
        2,
        adj.at[:, pl.ds(0, RMAX)],
        rims.at[1],
        adj.at[:, pl.ds(RMAX + rows, RMAX)],
        rims.at[0],
    )
    start_both(back)
    own_ref[...] = adj[:, RMAX : RMAX + rows]
    if rows > 2 * RMAX:
        rim_ref[...] = jnp.zeros_like(rim_ref)
    wait_both(back)
    rim_ref[:, :RMAX] = rims[0]
    rim_ref[:, rows - RMAX :] = rims[1]


def finish(power_ref, own_ref, rim_ref, resist_ref, grad_ref):
    resist_ref[...] = resist_of(power_ref[...])
    grad_ref[...] = own_ref[...] + rim_ref[...]


def on_device(mask_field, target, kernel_taps, kernel_radii, kernel_group, kernel_weight):
    rows, cols = target.shape
    kernels, _, taps, _ = kernel_taps.shape
    grid_rows, grid_cols = rows + taps, cols + taps
    consts = [jnp.asarray(t) for t in tables(rows, cols)]
    vmem = pl.BlockSpec(memory_space=pltpu.VMEM)
    smem = pl.BlockSpec(memory_space=pltpu.SMEM)
    hbm = pl.BlockSpec(memory_space=pltpu.HBM)
    plane = (grid_rows // 2, grid_cols // 2)
    intensity, own, rim = pl.pallas_call(
        body,
        out_shape=(
            jax.ShapeDtypeStruct((GROUPS, rows, cols), jnp.float32),
            jax.ShapeDtypeStruct((2, rows, cols), jnp.float32),
            jax.ShapeDtypeStruct((2, rows, cols), jnp.float32),
        ),
        in_specs=[smem] * 3 + [hbm] * (3 + len(consts)),
        out_specs=(vmem, vmem, vmem),
        scratch_shapes=[
            pltpu.VMEM((kernels, 8) + plane, jnp.float32),
            pltpu.VMEM((kernels, 2 * rows, cols), jnp.float32),
            pltpu.VMEM((8,) + plane, jnp.float32),
            pltpu.VMEM((GROUPS, rows, cols), jnp.float32),
            pltpu.VMEM(kernel_taps.shape, jnp.float32),
            pltpu.VMEM((2, grid_rows, cols), jnp.float32),
            pltpu.VMEM((rows, cols), jnp.int32),
            pltpu.VMEM((2, grid_rows, cols), jnp.float32),
            pltpu.VMEM((2, 2, RMAX, cols), jnp.float32),
        ]
        + [pltpu.VMEM(t.shape, t.dtype) for t in consts]
        + [
            pltpu.SemaphoreType.DMA((kernels,)),
            pltpu.SemaphoreType.DMA((10,)),
            pltpu.SemaphoreType.DMA((4,)),
            pltpu.SemaphoreType.DMA((4,)),
        ],
        compiler_params=pltpu.CompilerParams(
            vmem_limit_bytes=56 * 1024 * 1024, collective_id=0, has_side_effects=True
        ),
        name="litho",
    )(kernel_radii, kernel_group, kernel_weight, kernel_taps, mask_field, target, *consts)
    return pl.pallas_call(
        finish,
        out_shape=(
            jax.ShapeDtypeStruct((GROUPS, rows, cols), jnp.float32),
            jax.ShapeDtypeStruct((2, rows, cols), jnp.float32),
        ),
        in_specs=[vmem] * 3,
        out_specs=(vmem, vmem),
        name="finish",
    )(intensity, own, rim)


def solution(mesh):
    in_specs = (P(None, ("win", "row"), None), P(("win", "row"), None), P(), P(), P(), P())
    out_specs = (P(None, ("win", "row"), None), P(None, ("win", "row"), None))
    return jax.shard_map(
        on_device, mesh=mesh, in_specs=in_specs, out_specs=out_specs, check_vma=False
    )
```
